128 devices in a mesh: dp: 8 (over z_lo, x), mp: 16 (over z_hi, y, core).
Axes of the slice: x: 4, y: 4, z: 4 (z_hi: 2, z_lo: 2; z = z_hi * 2 + z_lo), core: 2. Of those that a mesh axis runs over, the one named last changes fastest.
Arguments:
- inputs: bfloat16 [256, 256, 3072], P('mp', None, 'dp'), may hold values from -6 to 6
- hidden_pre: bfloat16 [256, 256, 3072], P('mp', None, 'dp'), may hold values from -8 to 8
- cotangent: bfloat16 [256, 256, 3072], P('mp', None, 'dp'), may hold values from -6 to 6
- r1_weight: bfloat16 [256, 256, 256], P('mp'), may hold values from -0.375 to 0.375
- l1_weight: bfloat16 [256, 256, 256], P('mp'), may hold values from -0.375 to 0.375
- r2_weight: bfloat16 [256, 256, 256], P('mp'), may hold values from -0.375 to 0.375
- l2_weight: bfloat16 [256, 256, 256], P('mp'), may hold values from -0.375 to 0.375
Outputs:
- grad_inputs: bfloat16 [256, 256, 3072], P('mp', None, 'dp')
- grad_r1: float32 [256, 256, 256], P('mp', 'dp')
- grad_l1: float32 [256, 256, 256], P('mp', 'dp')
- grad_r2: float32 [256, 256, 256], P('mp', 'dp')
- grad_l2: float32 [256, 256, 256], P('mp', 'dp')
The draws below stay inside these ranges and needn't reach their ends.
All inputs are finite; a program needn't handle non-finite values.
Results may differ from the reference program's by a relative error of at most 0.008.
Values may be sent and summed in bfloat16 or wider, within the bound.
A program may use at most 128 MiB of HBM per device.

```python
import jax
import jax.numpy as jnp
from jax import lax

B = 256
TOK_DEV = 384
TOKENS = 3072
N_DP = 8


def raised(entries, own_key, source, target, parts, factor):
    owner, partner = [(jnp.arange(entries.shape[axis_at]) // (entries.shape[axis_at] // parts)).reshape([-1 if axis == axis_at else 1 for axis in range(entries.ndim)]) for axis_at in (source, target)]
    chosen = jax.random.permutation(own_key, parts)[partner]
    strong = (owner == chosen) | (owner == (partner + parts // 2) % parts)
    return jnp.where(strong, factor * entries, entries)


def levels(rng, shape, cuts, least, top_value):
    def one(axis_at, blocks):
        draws = jax.random.uniform(jax.random.fold_in(jax.random.fold_in(rng, 6), axis_at), (blocks,), jnp.float32, least / len(cuts), top_value / len(cuts))
        return jnp.repeat(jnp.exp(draws), shape[axis_at] // blocks).reshape((-1,) + (1,) * (len(shape) - axis_at - 1))

    loudness = one(*cuts[0])
    for cut in cuts[1:]:
        loudness = loudness * one(*cut)
    return loudness


def bell_draw(rng, shape, width, reach, cuts=(), dtype=jnp.bfloat16):
    level = levels(rng, shape, cuts, -0.22, 0.18) if cuts else 1.0
    values = jax.random.normal(rng, shape, jnp.float32) * width * level
    return jnp.minimum(jnp.maximum(values, -reach), reach).astype(dtype)


def heavy_noise(stream_key, dims, scale, most, cuts, heavy, dtype=jnp.bfloat16):
    entries = scale * jax.random.normal(stream_key, dims, jnp.float32)
    if cuts:
        entries = entries * levels(stream_key, dims, cuts, -0.22, 0.18)
    return jnp.clip(raised(entries, jax.random.fold_in(stream_key, 3), *heavy), -most, most).astype(dtype)


def setup_inputs(seed: int = 0) -> dict:
    streams_of = jax.random.split(jax.random.key(seed), 8)
    return {
        "inputs": heavy_noise(streams_of[0], (B, B, TOKENS), 1.0, 6.0, ((0, 16), (2, 8)), (2, 1, 8, 2.0)),
        "hidden_pre": heavy_noise(streams_of[1], (B, B, TOKENS), 1.5, 8.0, ((0, 16), (2, 8)), (2, 1, 8, 2.0)),
        "cotangent": bell_draw(streams_of[2], (B, B, TOKENS), 1.0, 6.0, ((0, 16), (2, 8))),
        "r1_weight": bell_draw(streams_of[3], (B, B, B), B ** -0.5, 0.375, ((0, 16),)),
        "l1_weight": bell_draw(streams_of[4], (B, B, B), B ** -0.5, 0.375, ((0, 16),)),
        "r2_weight": bell_draw(streams_of[5], (B, B, B), B ** -0.5, 0.375, ((0, 16),)),
        "l2_weight": bell_draw(streams_of[6], (B, B, B), B ** -0.5, 0.375, ((0, 16),)),
    }


def gelu_pair(value):
    coeff = 0.7978845608
    inner = coeff * (value + 0.044715 * value * value * value)
    tangent = jnp.tanh(inner)
    result = 0.5 * value * (1.0 + tangent)
    slope = 0.5 * (1.0 + tangent) + 0.5 * value * (1.0 - tangent * tangent) * coeff * (1.0 + 3.0 * 0.044715 * value * value)
    return result, slope


def mixed(form, left, right):
    return jnp.einsum(form, left.astype(jnp.float32), right.astype(jnp.float32))


def reference(inputs, hidden_pre, cotangent, r1_weight, l1_weight, r2_weight, l2_weight):
    def regroup(array):
        return jnp.moveaxis(array.reshape(B, B, N_DP, TOK_DEV), 2, 0)

    def group_pass(totals, pieces):
        tokens_in, hidden_in, grad_out = pieces
        r1_out = mixed("bio,bit->bot", r1_weight, tokens_in).astype(jnp.bfloat16)
        act_val, slope = gelu_pair(hidden_in.astype(jnp.float32))
        act = act_val.astype(jnp.bfloat16)
        r2_out = mixed("oqr,oqt->ort", r2_weight, act).astype(jnp.bfloat16)
        d_l2in = mixed("ros,rst->rot", l2_weight, grad_out).astype(jnp.bfloat16)
        part_l2 = mixed("ort,rst->ros", r2_out, grad_out).astype(jnp.bfloat16)
        part_r2 = mixed("oqt,rot->oqr", act, d_l2in).astype(jnp.bfloat16)
        d_hidden = (mixed("oqr,rot->oqt", r2_weight, d_l2in) * slope).astype(jnp.bfloat16)
        part_l1 = mixed("bot,oqt->obq", r1_out, d_hidden).astype(jnp.bfloat16)
        d_l1in = mixed("obq,oqt->obt", l1_weight, d_hidden).astype(jnp.bfloat16)
        part_r1 = mixed("bit,obt->bio", tokens_in, d_l1in).astype(jnp.bfloat16)
        grad_tokens = mixed("bio,obt->bit", r1_weight, d_l1in).astype(jnp.bfloat16)
        totals = (totals[0] + part_r1.astype(jnp.float32), totals[1] + part_l1.astype(jnp.float32),
                  totals[2] + part_r2.astype(jnp.float32), totals[3] + part_l2.astype(jnp.float32))
        return totals, grad_tokens

    zeros = jnp.zeros((B, B, B), jnp.float32)
    totals, grads = lax.scan(group_pass, (zeros, zeros, zeros, zeros),
                             (regroup(inputs), regroup(hidden_pre), regroup(cotangent)))
    grad_inputs = jnp.moveaxis(grads, 0, 2).reshape(B, B, N_DP * TOK_DEV)
    return (grad_inputs, totals[0], totals[1], totals[2], totals[3])
```

```python
import jax
import jax.numpy as jnp
from jax import lax
from jax.experimental import pallas as pl
from jax.experimental.pallas import tpu as pltpu
from jax.sharding import PartitionSpec as P

BF = jnp.bfloat16
F32 = jnp.float32
MESH = pl.DeviceIdType.MESH
NB, B, T = 16, 256, 384
CH = 4
NCH = NB // CH
LANES = 128
COEFF = 0.7978845608
D_L2IN, R1_OUT, D_L1IN, R2_OUT = range(4)
G_R2, G_L1, G_R1, G_L2 = range(4)


def dot(left, right, l_dim, r_dim):
    return lax.dot_general(
        left, right, (((l_dim,), (r_dim,)), ((), ())), preferred_element_type=F32
    )


def loop(count, step):
    lax.fori_loop(0, count, lambda i, carry: (step(i), carry)[1], 0)


def kernel(
    inp_h, hid_h, cot_h, r1_h, l1_h, r2_h, l2_h,
    ginp_h, gr1_h, gl1_h, gr2_h, gl2_h,
    inp, hid, cot, r1w, l1w, r2w, l2w,
    act, send, arrive, recv, part, xin, zout, zin, total, stage, prod,
    load_sem, out_sem, zs, zr, yo, yf, yr, xs, xr, ls, lr,
):
    d, m = lax.axis_index("dp"), lax.axis_index("mp")
    x, zl = d % 4, d // 4
    zh, yc = m // 8, m % 8
    y, core = yc // 2, yc % 2
    z_mate = (d, (1 - zh) * 8 + yc)
    l_mate = ((1 - zl) * 4 + x, m)
    near = []
    for dy, dc in ((2, 0), (2, 1), (1, 0), (3, 0), (1, 1), (3, 1), (0, 1)):
        near.append(((y + dy) % 4) * 2 + (core + dc) % 2)
    x_mates = [(zl * 4 + (x + dx) % 4, m) for dx in (1, 2, 3)]
    mate_m = (1 - zh) * 8 + yc

    loads = [
        pltpu.make_async_copy(src, dst, load_sem.at[i])
        for i, (src, dst) in enumerate(
            ((l2_h, l2w), (cot_h, cot), (r1_h, r1w), (inp_h, inp), (hid_h, hid), (r2_h, r2w), (l1_h, l1w))
        )
    ]
    for load in loads:
        load.start()

    barrier = pltpu.get_barrier_semaphore()
    mates = [z_mate, l_mate] + [(d, zh * 8 + n) for n in near] + x_mates
    for mate in mates:
        pl.semaphore_signal(barrier, inc=1, device_id=mate, device_id_type=MESH)

    def rows(c):
        return pl.ds(c * CH, CH)

    def remote(src, dst, s_sem, r_sem, device):
        return pltpu.make_async_remote_copy(
            src_ref=src, dst_ref=dst, send_sem=s_sem, recv_sem=r_sem, device_id=device, device_id_type=MESH
        )

    def await_bytes(ref, sem):
        pltpu.make_async_copy(ref, ref, sem).wait()

    def z_send(k, c):
        remote(
            send.at[k % 2, pl.ds((1 - zh) * 8, 8), rows(c)], arrive.at[k, :, rows(c)],
            zs.at[k, c], zr.at[k, c], z_mate,
        ).start()

    def y_own(k, c):
        for n in near:
            remote(
                send.at[k % 2, zh * 8 + n, rows(c)], recv.at[k, rows(c), m],
                yo.at[k, c], yr.at[k, c], (d, zh * 8 + n),
            ).start()
        pltpu.make_async_copy(send.at[k % 2, m, rows(c)], recv.at[k, rows(c), m], yr.at[k, c]).start()

    def y_forward(k, c):
        await_bytes(arrive.at[k, :, rows(c)], zr.at[k, c])
        for n in near:
            remote(
                arrive.at[k, n, rows(c)], recv.at[k, rows(c), mate_m],
                yf.at[k, c], yr.at[k, c], (d, zh * 8 + n),
            ).start()
        pltpu.make_async_copy(arrive.at[k, yc, rows(c)], recv.at[k, rows(c), mate_m], yr.at[k, c]).start()

    def arrived(k, c):
        await_bytes(recv.at[k, rows(c)], yr.at[k, c])

    def sends_done(k, c):
        await_bytes(arrive.at[k, :, rows(c)], zs.at[k, c])
        await_bytes(arrive.at[k, pl.ds(0, 7), rows(c)], yo.at[k, c])
        await_bytes(arrive.at[k, pl.ds(0, 7), rows(c)], yf.at[k, c])

    def produce(k, weight, w_dim, data):
        def span(tc):
            lanes = pl.ds(pl.multiple_of(tc * LANES, LANES), LANES)

            def block(j):
                stage[pl.ds(j, B, stride=NB), :] = dot(weight[j], data[j, :, lanes], w_dim, 0)

            def pack(dest):
                rows_of = pl.ds(pl.multiple_of(dest * B, B), B)
                send[k % 2, dest, :, :, lanes] = stage[rows_of, :].astype(BF).reshape(NB, NB, LANES)

            loop(NB, block)
            loop(NB, pack)

        loop(T // LANES, span)

    def received(k, j):
        return recv[k, j].reshape(B, T)

    def gradient(g, j, value):
        part[g % 2, j] = value.astype(BF).reshape(2, 4, 32, B)

    def x_send(g, c):
        for i, mate in enumerate(x_mates):
            remote(
                part.at[g % 2, rows(c), :, (x + i + 1) % 4], xin.at[g, i, rows(c)],
                xs.at[g, c], xr.at[g, c], mate,
            ).start()

    def x_done(g, c):
        await_bytes(xin.at[g, :, rows(c)], xs.at[g, c])

    def x_sum(g, c):
        await_bytes(xin.at[g, :, rows(c)], xr.at[g, c])

        def block(i):
            j = c * CH + i

            def joined(half):
                value = part[g % 2, j, half, x].astype(F32)
                for s in range(3):
                    value += xin[g, s, j, half].astype(F32)
                return value

            zout[g, j] = joined(1 - zl).astype(BF)
            total[g, j] = joined(zl)

        loop(CH, block)
        remote(zout.at[g, rows(c)], zin.at[g, rows(c)], ls.at[g, c], lr.at[g, c], l_mate).start()

    grads_h = {G_R2: gr2_h, G_L1: gl1_h, G_R1: gr1_h, G_L2: gl2_h}

    def finish(g, c):
        await_bytes(zin.at[g, rows(c)], lr.at[g, c])

        def block(i):
            j = c * CH + i
            total[g, j] += zin[g, j].astype(F32)

        loop(CH, block)
        pltpu.make_async_copy(total.at[g, rows(c)], grads_h[g].at[rows(c)], out_sem.at[g, c]).start()

    def gelu_block(j):
        def group(i):
            span = pl.ds(pl.multiple_of(i * 32, 32), 32)
            v = hid[j, span, :].astype(F32)
            t = jnp.tanh(COEFF * (v + 0.044715 * v * v * v))
            act[j, span, :] = (0.5 * v * (1.0 + t)).astype(BF)

        loop(B // 32, group)

    def d_hidden_block(j):
        prod[...] = dot(r2w[j], received(D_L2IN, j), 1, 0)

        def group(i):
            span = pl.ds(pl.multiple_of(i * 32, 32), 32)
            v = hid[j, span, :].astype(F32)
            t = jnp.tanh(COEFF * (v + 0.044715 * v * v * v))
            slope = 0.5 * (1.0 + t) + 0.5 * v * (1.0 - t * t) * COEFF * (1.0 + 3.0 * 0.044715 * v * v)
            hid[j, span, :] = (prod[span, :] * slope).astype(BF)

        loop(B // 32, group)

    def each(c, step):
        loop(CH, lambda i: step(c * CH + i))

    loads[0].wait()
    loads[1].wait()
    produce(D_L2IN, l2w, 1, cot)
    pl.semaphore_wait(barrier, len(mates))
    loop(NCH, lambda c: z_send(D_L2IN, c))
    loop(NCH, lambda c: y_own(D_L2IN, c))
    loads[2].wait()
    loads[3].wait()
    produce(R1_OUT, r1w, 0, inp)
    loads[4].wait()

    def step(c):
        y_forward(D_L2IN, c)
        z_send(R1_OUT, c)
        y_own(R1_OUT, c)
        each(c, gelu_block)

    loop(NCH, step)
    loads[5].wait()

    def step(c):
        arrived(D_L2IN, c)
        each(c, d_hidden_block)
        each(c, lambda j: gradient(G_R2, j, dot(act[j], received(D_L2IN, j), 1, 1)))
        x_send(G_R2, c)

    loop(NCH, step)
    loads[6].wait()
    loop(NCH, lambda c: sends_done(D_L2IN, c))
    produce(D_L1IN, l1w, 1, hid)

    def step(c):
        y_forward(R1_OUT, c)
        z_send(D_L1IN, c)
        y_own(D_L1IN, c)
        x_sum(G_R2, c)

    loop(NCH, step)
    def step(c):
        arrived(R1_OUT, c)
        each(c, lambda j: gradient(G_L1, j, dot(received(R1_OUT, j), hid[j], 1, 1)))
        x_send(G_L1, c)

    loop(NCH, step)
    loop(NCH, lambda c: sends_done(R1_OUT, c))
    produce(R2_OUT, r2w, 0, act)

    def step(c):
        y_forward(D_L1IN, c)
        z_send(R2_OUT, c)
        y_own(R2_OUT, c)
        finish(G_R2, c)
        x_sum(G_L1, c)
        x_done(G_R2, c)

    loop(NCH, step)
    def step(c):
        arrived(D_L1IN, c)
        each(c, lambda j: gradient(G_R1, j, dot(inp[j], received(D_L1IN, j), 1, 1)))
        x_send(G_R1, c)

        def data_gradient(j):
            act[j] = dot(r1w[j], received(D_L1IN, j), 1, 0).astype(BF)

        each(c, data_gradient)
        pltpu.make_async_copy(act.at[rows(c)], ginp_h.at[rows(c)], load_sem.at[7 + c]).start()

    loop(NCH, step)
    def step(c):
        y_forward(R2_OUT, c)
        finish(G_L1, c)
        x_done(G_L1, c)
        x_sum(G_R1, c)

    loop(NCH, step)

    def step(c):
        arrived(R2_OUT, c)
        each(c, lambda j: gradient(G_L2, j, dot(received(R2_OUT, j), cot[j], 1, 1)))
        x_send(G_L2, c)

    loop(NCH, step)

    def step(c):
        x_sum(G_L2, c)
        finish(G_R1, c)

    loop(NCH, step)

    def step(c):
        finish(G_L2, c)
        sends_done(D_L1IN, c)
        sends_done(R2_OUT, c)
        x_done(G_R1, c)
        x_done(G_L2, c)
        pltpu.make_async_copy(act.at[rows(c)], ginp_h.at[rows(c)], load_sem.at[7 + c]).wait()
        for g in range(4):
            await_bytes(zout.at[g, rows(c)], ls.at[g, c])
            pltpu.make_async_copy(total.at[g, rows(c)], grads_h[g].at[rows(c)], out_sem.at[g, c]).wait()

    loop(NCH, step)


def body(inputs, hidden_pre, cotangent, r1_weight, l1_weight, r2_weight, l2_weight):
    anywhere = pl.BlockSpec(memory_space=pl.ANY)
    vmem, dma = pltpu.VMEM, pltpu.SemaphoreType.DMA
    grad = jax.ShapeDtypeStruct((NB, 32, B), F32)
    wide, square = (NB, B, T), (NB, B, B)
    return pl.pallas_call(
        kernel,
        name="monarch_backward",
        out_shape=(jax.ShapeDtypeStruct(wide, BF), grad, grad, grad, grad),
        in_specs=[anywhere] * 7,
        out_specs=(anywhere,) * 5,
        scratch_shapes=[
            vmem(wide, BF), vmem(wide, BF), vmem(wide, BF),
            vmem(square, BF), vmem(square, BF), vmem(square, BF), vmem(square, BF),
            vmem(wide, BF),
            vmem((2, 16, NB, NB, T), BF),
            vmem((4, 8, NB, NB, T), BF),
            vmem((4, NB, 16, NB, T), BF),
            vmem((2, NB, 2, 4, 32, B), BF),
            vmem((4, 3, NB, 2, 32, B), BF),
            vmem((4, NB, 32, B), BF),
            vmem((4, NB, 32, B), BF),
            vmem((4, NB, 32, B), F32),
            vmem((NB * B, LANES), F32),
            vmem((B, T), F32),
            dma((7 + NCH,)),
        ]
        + [dma((4, NCH))] * 10,
        compiler_params=pltpu.CompilerParams(
            collective_id=0, has_side_effects=True, vmem_limit_bytes=67_000_000
        ),
    )(inputs, hidden_pre, cotangent, r1_weight, l1_weight, r2_weight, l2_weight)


def solution(mesh):
    act_spec, weight = P("mp", None, "dp"), P("mp", None, None)
    return jax.shard_map(
        body,
        mesh=mesh,
        in_specs=(act_spec,) * 3 + (weight,) * 4,
        out_specs=(act_spec,) + (P("mp", "dp", None),) * 4,
        check_vma=False,
    )
```

```python
import jax
import jax.numpy as jnp
from jax import lax
from jax.experimental import pallas as pl
from jax.experimental.pallas import tpu as pltpu
from jax.sharding import PartitionSpec as P

BF = jnp.bfloat16
F32 = jnp.float32
MESH = pl.DeviceIdType.MESH
NB, B, T = 16, 256, 384
LANES = 128
COEFF = 0.7978845608
D_L2IN, D_L1IN, R1_OUT, R2_OUT = range(4)
G_R2, G_R1, G_L1, G_L2 = range(4)
LANE_CHUNKS = (True, True, False, False)
CHUNKS = (3, 3, 4, 8)
SLOT = (0, 1, 2, 0)
SUMS = (4, 4, 4, 8)


def dot(left, right, l_dim, r_dim):
    return lax.dot_general(
        left, right, (((l_dim,), (r_dim,)), ((), ())), preferred_element_type=F32
    )


def loop(count, step, unroll=1):
    lax.fori_loop(0, count, lambda i, carry: (step(i), carry)[1], 0, unroll=4 if count == NB else unroll)


def kernel(
    inp_h, hid_h, cot_h, r1_h, l1_h, r2_h, l2_h,
    ginp_h, gr1_h, gl1_h, gr2_h, gl2_h,
    inp, hid, cot, r1w, r2w, l_w,
    act, send, arrive, recv, part, xin, zout, zin, total, stage,
    load_sem, out_sem, zs, zr, yo, yf, yr, xs, xr, ls, lr,
):
    d, m = lax.axis_index("dp"), lax.axis_index("mp")
    x, zl = d % 4, d // 4
    zh, yc = m // 8, m % 8
    y, core = yc // 2, yc % 2
    z_mate = (d, (1 - zh) * 8 + yc)
    l_mate = ((1 - zl) * 4 + x, m)
    near = []
    for dy, dc in ((2, 0), (2, 1), (1, 0), (3, 0), (1, 1), (3, 1), (0, 1)):
        near.append(((y + dy) % 4) * 2 + (core + dc) % 2)
    x_mates = [(zl * 4 + (x + dx) % 4, m) for dx in (1, 2, 3)]
    mate_m = (1 - zh) * 8 + yc

    def load(i, src, dst):
        return pltpu.make_async_copy(src, dst, load_sem.at[i])

    def cot_part(tc):
        span = pl.ds(tc * LANES, LANES)
        return load(tc, cot_h.at[:, :, span], cot.at[:, :, span])

    first = [load(3, l2_h, l_w), cot_part(0), cot_part(1), cot_part(2)]
    later = [
        load(i + 4, src, dst)
        for i, (src, dst) in enumerate(((r1_h, r1w), (inp_h, inp), (hid_h, hid), (r2_h, r2w)))
    ]
    last = load(8, l1_h, l_w)
    for copy in first:
        copy.start()

    barrier = pltpu.get_barrier_semaphore()
    mates = [z_mate, l_mate] + [(d, zh * 8 + n) for n in near] + x_mates
    for mate in mates:
        pl.semaphore_signal(barrier, inc=1, device_id=mate, device_id_type=MESH)

    def rows(k, c):
        if LANE_CHUNKS[k]:
            return pl.ds(0, NB)
        return pl.ds(c * (NB // CHUNKS[k]), NB // CHUNKS[k])

    def lanes(k, c):
        if LANE_CHUNKS[k]:
            return pl.ds(pl.multiple_of(c * LANES, LANES), LANES)
        return pl.ds(0, T)

    def remote(src, dst, s_sem, r_sem, device):
        return pltpu.make_async_remote_copy(
            src_ref=src, dst_ref=dst, send_sem=s_sem, recv_sem=r_sem, device_id=device, device_id_type=MESH
        )

    def await_bytes(ref, sem):
        pltpu.make_async_copy(ref, ref, sem).wait()

    def z_send(k, c):
        remote(
            send.at[SLOT[k], pl.ds((1 - zh) * 8, 8), rows(k, c), :, lanes(k, c)],
            arrive.at[k, :, rows(k, c), :, lanes(k, c)],
            zs.at[k, c], zr.at[k, c], z_mate,
        ).start()

    def y_own(k, c):
        here = recv.at[k, rows(k, c), m, :, lanes(k, c)]
        for n in near:
            remote(
                send.at[SLOT[k], zh * 8 + n, rows(k, c), :, lanes(k, c)], here,
                yo.at[k, c], yr.at[k, c], (d, zh * 8 + n),
            ).start()
        pltpu.make_async_copy(
            send.at[SLOT[k], m, rows(k, c), :, lanes(k, c)], here, yr.at[k, c]
        ).start()

    def dispatch(k, c):
        z_send(k, c)
        y_own(k, c)

    def forward(k, c):
        await_bytes(arrive.at[k, :, rows(k, c), :, lanes(k, c)], zr.at[k, c])
        here = recv.at[k, rows(k, c), mate_m, :, lanes(k, c)]
        for n in near:
            remote(
                arrive.at[k, n, rows(k, c), :, lanes(k, c)], here,
                yf.at[k, c], yr.at[k, c], (d, zh * 8 + n),
            ).start()
        pltpu.make_async_copy(arrive.at[k, yc, rows(k, c), :, lanes(k, c)], here, yr.at[k, c]).start()

    def arrived(k, c):
        await_bytes(recv.at[k, rows(k, c), :, :, lanes(k, c)], yr.at[k, c])

    def sends_done(k):
        def step(c):
            seven = arrive.at[k, pl.ds(0, 7), rows(k, c), :, lanes(k, c)]
            await_bytes(arrive.at[k, :, rows(k, c), :, lanes(k, c)], zs.at[k, c])
            await_bytes(seven, yo.at[k, c])
            await_bytes(seven, yf.at[k, c])

        loop(CHUNKS[k], step)

    def produce(k, tc, weight, w_dim, data):
        span = pl.ds(pl.multiple_of(tc * LANES, LANES), LANES)

        def block(j):
            stage[pl.ds(j, B, stride=NB), :] = dot(weight[j], data[j, :, span], w_dim, 0)

        def pack(dest):
            rows_of = pl.ds(pl.multiple_of(dest * B, B), B)
            send[SLOT[k], dest, :, :, span] = stage[rows_of, :].astype(BF).reshape(NB, NB, LANES)

        loop(NB, block)
        loop(NB, pack)

    def received(k, j):
        return recv[k, j].reshape(B, T)

    def piece(g, c):
        return pl.ds(c * (NB // SUMS[g]), NB // SUMS[g])

    def each(g, c, step):
        loop(NB // SUMS[g], lambda i: step(c * (NB // SUMS[g]) + i), NB // SUMS[g])

    def gradient(g, c, product):
        def block(j):
            part[g % 2, j] = product(j).astype(BF).reshape(2, 4, 32, B)

        each(g, c, block)
        for i, mate in enumerate(x_mates):
            remote(
                part.at[g % 2, piece(g, c), :, (x + i + 1) % 4], xin.at[g, i, piece(g, c)],
                xs.at[g, c], xr.at[g, c], mate,
            ).start()

    def x_done(g):
        loop(SUMS[g], lambda c: await_bytes(xin.at[g, :, piece(g, c)], xs.at[g, c]))

    def x_sum(g, c):
        await_bytes(xin.at[g, :, piece(g, c)], xr.at[g, c])

        def block(j):
            def joined(half):
                value = part[g % 2, j, half, x].astype(F32)
                for s in range(3):
                    value += xin[g, s, j, half].astype(F32)
                return value

            zout[g, j] = joined(1 - zl).astype(BF)
            total[g, j] = joined(zl)

        each(g, c, block)
        remote(zout.at[g, piece(g, c)], zin.at[g, piece(g, c)], ls.at[g, c], lr.at[g, c], l_mate).start()

    grads_h = {G_R2: gr2_h, G_L1: gl1_h, G_R1: gr1_h, G_L2: gl2_h}

    def out_copy(g, c):
        return pltpu.make_async_copy(total.at[g, piece(g, c)], grads_h[g].at[piece(g, c)], out_sem.at[g, c])

    def finish(g, c):
        await_bytes(zin.at[g, piece(g, c)], lr.at[g, c])

        def block(j):
            total[g, j] += zin[g, j].astype(F32)

        each(g, c, block)
        out_copy(g, c).start()

    def gelu_parts(v):
        return v, jnp.tanh(COEFF * (v + 0.044715 * v * v * v))

    def gelu_block(j):
        def group(i):
            span = pl.ds(pl.multiple_of(i * 32, 32), 32)
            v, t = gelu_parts(hid[j, span, :].astype(F32))
            act[j, span, :] = (0.5 * v * (1.0 + t)).astype(BF)

        loop(B // 32, group)

    def d_hidden(tc):
        span = pl.ds(pl.multiple_of(tc * LANES, LANES), LANES)

        def block(j):
            v, t = gelu_parts(hid[j, :, span].astype(F32))
            slope = 0.5 * (1.0 + t) + 0.5 * v * (1.0 - t * t) * COEFF * (1.0 + 3.0 * 0.044715 * v * v)
            back = dot(r2w[j], recv[D_L2IN, j, :, :, span].reshape(B, LANES), 1, 0)
            hid[j, :, span] = (back * slope).astype(BF)

        loop(NB, block)

    def grad_r2(c):
        gradient(G_R2, c, lambda j: dot(act[j], received(D_L2IN, j), 1, 1))

    def grad_r1(c):
        gradient(G_R1, c, lambda j: dot(inp[j], received(D_L1IN, j), 1, 1))

    def grad_l1(c):
        gradient(G_L1, c, lambda j: dot(received(R1_OUT, j), hid[j], 1, 1))

    def grad_l2(c):
        gradient(G_L2, c, lambda j: dot(received(R2_OUT, j), cot[j], 1, 1))

    def out_inputs(c):
        return pltpu.make_async_copy(act.at[pl.ds(c * 4, 4)], ginp_h.at[pl.ds(c * 4, 4)], load_sem.at[9 + c])

    def grad_inputs(c):
        def block(i):
            act[c * 4 + i] = dot(r1w[c * 4 + i], received(D_L1IN, c * 4 + i), 1, 0).astype(BF)

        loop(4, block, 4)
        out_inputs(c).start()

    for tc in range(3):
        if tc == 0:
            first[0].wait()
        first[1 + tc].wait()
        if tc == 1:
            for copy in later:
                copy.start()
        produce(D_L2IN, tc, l_w, 1, cot)
        if tc == 0:
            pl.semaphore_wait(barrier, len(mates))
        dispatch(D_L2IN, tc)
    last.start()
    later[0].wait()
    later[1].wait()
    loop(3, lambda tc: produce(R1_OUT, tc, r1w, 0, inp))
    later[2].wait()
    loop(NB, gelu_block)
    later[3].wait()
    last.wait()

    forward(D_L2IN, 0)

    def step(c):
        arrived(D_L2IN, c)
        d_hidden(c)
        produce(D_L1IN, c, l_w, 1, hid)
        dispatch(D_L1IN, c)

    def follow(c):
        step(c)
        forward(D_L2IN, c + 1)

    loop(2, follow)
    step(2)
    forward(D_L1IN, 0)
    loop(4, grad_r2)
    sends_done(D_L2IN)
    loop(3, lambda tc: produce(R2_OUT, tc, r2w, 0, act))
    forward(D_L1IN, 1)
    dispatch(R1_OUT, 0)
    dispatch(R1_OUT, 1)
    x_sum(G_R2, 0)
    x_sum(G_R2, 1)
    forward(D_L1IN, 2)
    dispatch(R1_OUT, 2)
    dispatch(R1_OUT, 3)
    x_sum(G_R2, 2)
    x_sum(G_R2, 3)
    loop(8, lambda c: z_send(R2_OUT, c))
    loop(3, lambda c: arrived(D_L1IN, c))
    x_done(G_R2)
    loop(4, grad_r1)
    forward(R1_OUT, 0)
    loop(4, grad_inputs)
    forward(R1_OUT, 1)
    y_own(R2_OUT, 0)
    y_own(R2_OUT, 1)
    x_sum(G_R1, 0)
    x_sum(G_R1, 1)
    arrived(R1_OUT, 0)
    grad_l1(0)
    forward(R1_OUT, 2)
    y_own(R2_OUT, 2)
    y_own(R2_OUT, 3)
    x_sum(G_R1, 2)
    x_sum(G_R1, 3)
    arrived(R1_OUT, 1)
    grad_l1(1)
    forward(R1_OUT, 3)
    y_own(R2_OUT, 4)
    x_done(G_R1)
    arrived(R1_OUT, 2)
    grad_l1(2)
    x_sum(G_L1, 0)
    forward(R2_OUT, 0)
    y_own(R2_OUT, 5)
    arrived(R1_OUT, 3)
    grad_l1(3)
    x_sum(G_L1, 1)

    forward(R2_OUT, 1)
    y_own(R2_OUT, 6)
    arrived(R2_OUT, 0)
    grad_l2(0)
    x_sum(G_L1, 2)
    forward(R2_OUT, 2)
    y_own(R2_OUT, 7)
    arrived(R2_OUT, 1)
    grad_l2(1)
    x_sum(G_L1, 3)

    def step(c):
        forward(R2_OUT, c)
        arrived(R2_OUT, c - 1)
        grad_l2(c - 1)
        x_sum(G_L2, c - 3)

    lax.fori_loop(3, 8, lambda c, carry: (step(c), carry)[1], 0)
    x_sum(G_L2, 5)
    arrived(R2_OUT, 7)
    grad_l2(7)
    loop(4, lambda c: finish(G_R2, c))
    x_sum(G_L2, 6)
    x_sum(G_L2, 7)
    for g in (G_R1, G_L1, G_L2):
        loop(SUMS[g], lambda c, g=g: finish(g, c))

    for k in (D_L1IN, R1_OUT, R2_OUT):
        sends_done(k)
    x_done(G_L1)
    x_done(G_L2)
    loop(4, lambda c: out_inputs(c).wait())
    for g in range(4):

        def step(c, g=g):
            await_bytes(zout.at[g, piece(g, c)], ls.at[g, c])
            out_copy(g, c).wait()

        loop(SUMS[g], step)


def deliver(*refs):
    srcs, outs, bufs, (s_in, s_out) = refs[:5], refs[5:10], refs[10:15], refs[15:]
    parts = [(0, pl.ds(c * 4, 4)) for c in range(4)] + [(i, pl.ds(0, NB)) for i in range(1, 5)]
    reads = [
        pltpu.make_async_copy(srcs[i].at[p], bufs[i].at[p], s_in.at[n]) for n, (i, p) in enumerate(parts)
    ]
    writes = [
        pltpu.make_async_copy(bufs[i].at[p], outs[i].at[p], s_out.at[n]) for n, (i, p) in enumerate(parts)
    ]
    for read in reads:
        read.start()
    for read, write in zip(reads, writes):
        read.wait()
        write.start()
    for write in writes:
        write.wait()


def body(inputs, hidden_pre, cotangent, r1_weight, l1_weight, r2_weight, l2_weight):
    anywhere = pl.BlockSpec(memory_space=pl.ANY)
    vmem, dma = pltpu.VMEM, pltpu.SemaphoreType.DMA
    grad = jax.ShapeDtypeStruct((NB, 32, B), F32)
    wide, square = (NB, B, T), (NB, B, B)
    results = pl.pallas_call(
        kernel,
        name="monarch_backward",
        out_shape=(jax.ShapeDtypeStruct(wide, BF), grad, grad, grad, grad),
        in_specs=[anywhere] * 7,
        out_specs=(anywhere,) * 5,
        scratch_shapes=[
            vmem(wide, BF), vmem(wide, BF), vmem(wide, BF),
            vmem(square, BF), vmem(square, BF), vmem(square, BF),
            vmem(wide, BF),
            vmem((3, 16, NB, NB, T), BF),
            vmem((4, 8, NB, NB, T), BF),
            vmem((4, NB, 16, NB, T), BF),
            vmem((2, NB, 2, 4, 32, B), BF),
            vmem((4, 3, NB, 2, 32, B), BF),
            vmem((4, NB, 32, B), BF),
            vmem((4, NB, 32, B), BF),
            vmem((4, NB, 32, B), F32),
            vmem((NB * B, LANES), F32),
            dma((13,)),
        ]
        + [dma((4, 8))] * 10,
        compiler_params=pltpu.CompilerParams(
            collective_id=0, has_side_effects=True, vmem_limit_bytes=67_000_000
        ),
    )(inputs, hidden_pre, cotangent, r1_weight, l1_weight, r2_weight, l2_weight)
    shapes = tuple(jax.ShapeDtypeStruct(r.shape, r.dtype) for r in results)
    return pl.pallas_call(
        deliver,
        name="deliver",
        out_shape=shapes,
        in_specs=[anywhere] * 5,
        out_specs=(anywhere,) * 5,
        scratch_shapes=[vmem(r.shape, r.dtype) for r in results] + [dma((8,)), dma((8,))],
        compiler_params=pltpu.CompilerParams(vmem_limit_bytes=67_000_000),
    )(*results)


def solution(mesh):
    act_spec, weight = P("mp", None, "dp"), P("mp", None, None)
    return jax.shard_map(
        body,
        mesh=mesh,
        in_specs=(act_spec,) * 3 + (weight,) * 4,
        out_specs=(act_spec,) + (P("mp", "dp", None),) * 4,
        check_vma=False,
    )
```

```python
import jax
import jax.numpy as jnp
from jax import lax
from jax.experimental import pallas as pl
from jax.experimental.pallas import tpu as pltpu
from jax.sharding import PartitionSpec as P

BF = jnp.bfloat16
F32 = jnp.float32
MESH = pl.DeviceIdType.MESH
NB, B, T = 16, 256, 384
LANES = 128
COEFF = 0.7978845608
D_L2IN, D_L1IN, R1_OUT, R2_OUT = range(4)
G_R2, G_R1, G_L1, G_L2 = range(4)
LANE_CHUNKS = (True, True, False, False)
CHUNKS = (3, 3, 4, 8)
SLOT = (0, 1, 2, 0)
SUMS = (4, 4, 4, 8)


def dot(left, right, l_dim, r_dim):
    return lax.dot_general(
        left, right, (((l_dim,), (r_dim,)), ((), ())), preferred_element_type=F32
    )


def loop(count, step, unroll=1):
    lax.fori_loop(0, count, lambda i, carry: (step(i), carry)[1], 0, unroll=4 if count == NB else unroll)


def kernel(
    inp_h, hid_h, cot_h, r1_h, l1_h, r2_h, l2_h,
    ginp_h, gr1_h, gl1_h, gr2_h, gl2_h,
    inp, hid, cot, r1w, r2w, l_w,
    act, send, arrive, recv, part, xin, zout, zin, total, stage,
    load_sem, out_sem, zs, zr, yo, yf, yr, xs, xr, ls, lr,
):
    d, m = lax.axis_index("dp"), lax.axis_index("mp")
    x, zl = d % 4, d // 4
    zh, yc = m // 8, m % 8
    y, core = yc // 2, yc % 2
    z_mate = (d, (1 - zh) * 8 + yc)
    l_mate = ((1 - zl) * 4 + x, m)
    near = []
    for dy, dc in ((2, 0), (2, 1), (1, 0), (3, 0), (1, 1), (3, 1), (0, 1)):
        near.append(((y + dy) % 4) * 2 + (core + dc) % 2)
    x_mates = [(zl * 4 + (x + dx) % 4, m) for dx in (1, 2, 3)]
    mate_m = (1 - zh) * 8 + yc

    def load(i, src, dst):
        return pltpu.make_async_copy(src, dst, load_sem.at[i])

    def cot_part(tc):
        span = pl.ds(tc * LANES, LANES)
        return load(tc, cot_h.at[:, :, span], cot.at[:, :, span])

    first = [load(3, l2_h, l_w), cot_part(0), cot_part(1), cot_part(2)]
    later = [
        load(i + 4, src, dst)
        for i, (src, dst) in enumerate(((r1_h, r1w), (inp_h, inp), (hid_h, hid), (r2_h, r2w)))
    ]
    last = load(8, l1_h, l_w)
    for copy in first:
        copy.start()

    barrier = pltpu.get_barrier_semaphore()
    mates = [z_mate, l_mate] + [(d, zh * 8 + n) for n in near] + x_mates
    for mate in mates:
        pl.semaphore_signal(barrier, inc=1, device_id=mate, device_id_type=MESH)

    def rows(k, c):
        if LANE_CHUNKS[k]:
            return pl.ds(0, NB)
        return pl.ds(c * (NB // CHUNKS[k]), NB // CHUNKS[k])

    def lanes(k, c):
        if LANE_CHUNKS[k]:
            return pl.ds(pl.multiple_of(c * LANES, LANES), LANES)
        return pl.ds(0, T)

    def remote(src, dst, s_sem, r_sem, device):
        return pltpu.make_async_remote_copy(
            src_ref=src, dst_ref=dst, send_sem=s_sem, recv_sem=r_sem, device_id=device, device_id_type=MESH
        )

    def await_bytes(ref, sem):
        pltpu.make_async_copy(ref, ref, sem).wait()

    def z_send(k, c):
        remote(
            send.at[SLOT[k], pl.ds((1 - zh) * 8, 8), rows(k, c), :, lanes(k, c)],
            arrive.at[k, :, rows(k, c), :, lanes(k, c)],
            zs.at[k, c], zr.at[k, c], z_mate,
        ).start()

    def y_own(k, c):
        here = recv.at[k, rows(k, c), m, :, lanes(k, c)]
        for n in near:
            remote(
                send.at[SLOT[k], zh * 8 + n, rows(k, c), :, lanes(k, c)], here,
                yo.at[k, c], yr.at[k, c], (d, zh * 8 + n),
            ).start()
        pltpu.make_async_copy(
            send.at[SLOT[k], m, rows(k, c), :, lanes(k, c)], here, yr.at[k, c]
        ).start()

    def dispatch(k, c):
        z_send(k, c)
        y_own(k, c)

    def forward(k, c):
        await_bytes(arrive.at[k, :, rows(k, c), :, lanes(k, c)], zr.at[k, c])
        here = recv.at[k, rows(k, c), mate_m, :, lanes(k, c)]
        for n in near:
            remote(
                arrive.at[k, n, rows(k, c), :, lanes(k, c)], here,
                yf.at[k, c], yr.at[k, c], (d, zh * 8 + n),
            ).start()
        pltpu.make_async_copy(arrive.at[k, yc, rows(k, c), :, lanes(k, c)], here, yr.at[k, c]).start()

    def arrived(k, c):
        await_bytes(recv.at[k, rows(k, c), :, :, lanes(k, c)], yr.at[k, c])

    def sends_done(k):
        def step(c):
            seven = arrive.at[k, pl.ds(0, 7), rows(k, c), :, lanes(k, c)]
            await_bytes(arrive.at[k, :, rows(k, c), :, lanes(k, c)], zs.at[k, c])
            await_bytes(seven, yo.at[k, c])
            await_bytes(seven, yf.at[k, c])

        loop(CHUNKS[k], step)

    def produce(k, tc, weight, w_dim, data):
        span = pl.ds(pl.multiple_of(tc * LANES, LANES), LANES)

        def block(j):
            stage[pl.ds(j, B, stride=NB), :] = dot(weight[j], data[j, :, span], w_dim, 0)

        def pack(dest):
            rows_of = pl.ds(pl.multiple_of(dest * B, B), B)
            send[SLOT[k], dest, :, :, span] = stage[rows_of, :].astype(BF).reshape(NB, NB, LANES)

        loop(NB, block)
        loop(NB, pack)

    def received(k, j):
        return recv[k, j].reshape(B, T)

    def piece(g, c):
        return pl.ds(c * (NB // SUMS[g]), NB // SUMS[g])

    def each(g, c, step):
        loop(NB // SUMS[g], lambda i: step(c * (NB // SUMS[g]) + i), NB // SUMS[g])

    def gradient(g, c, product):
        def block(j):
            part[g % 2, j] = product(j).astype(BF).reshape(2, 4, 32, B)

        each(g, c, block)
        for i, mate in enumerate(x_mates):
            remote(
                part.at[g % 2, piece(g, c), :, (x + i + 1) % 4], xin.at[g, i, piece(g, c)],
                xs.at[g, c], xr.at[g, c], mate,
            ).start()

    def x_done(g):
        loop(SUMS[g], lambda c: await_bytes(xin.at[g, :, piece(g, c)], xs.at[g, c]))

    def x_sum(g, c):
        await_bytes(xin.at[g, :, piece(g, c)], xr.at[g, c])

        def block(j):
            def joined(half):
                value = part[g % 2, j, half, x].astype(F32)
                for s in range(3):
                    value += xin[g, s, j, half].astype(F32)
                return value

            zout[g, j] = joined(1 - zl).astype(BF)
            total[g, j] = joined(zl)

        each(g, c, block)
        remote(zout.at[g, piece(g, c)], zin.at[g, piece(g, c)], ls.at[g, c], lr.at[g, c], l_mate).start()

    grads_h = {G_R2: gr2_h, G_L1: gl1_h, G_R1: gr1_h, G_L2: gl2_h}

    def out_copy(g, c):
        return pltpu.make_async_copy(total.at[g, piece(g, c)], grads_h[g].at[piece(g, c)], out_sem.at[g, c])

    def finish(g, c):
        await_bytes(zin.at[g, piece(g, c)], lr.at[g, c])

        def block(j):
            total[g, j] += zin[g, j].astype(F32)

        each(g, c, block)
        out_copy(g, c).start()

    def gelu_parts(v):
        return v, jnp.tanh(COEFF * (v + 0.044715 * v * v * v))

    def gelu_block(j):
        def group(i):
            span = pl.ds(pl.multiple_of(i * 32, 32), 32)
            v, t = gelu_parts(hid[j, span, :].astype(F32))
            act[j, span, :] = (0.5 * v * (1.0 + t)).astype(BF)

        loop(B // 32, group)

    def d_hidden(tc):
        span = pl.ds(pl.multiple_of(tc * LANES, LANES), LANES)

        def block(j):
            v, t = gelu_parts(hid[j, :, span].astype(F32))
            slope = 0.5 * (1.0 + t) + 0.5 * v * (1.0 - t * t) * COEFF * (1.0 + 3.0 * 0.044715 * v * v)
            back = dot(r2w[j], recv[D_L2IN, j, :, :, span].reshape(B, LANES), 1, 0)
            hid[j, :, span] = (back * slope).astype(BF)

        loop(NB, block)

    def grad_r2(c):
        gradient(G_R2, c, lambda j: dot(act[j], received(D_L2IN, j), 1, 1))

    def grad_r1(c):
        gradient(G_R1, c, lambda j: dot(inp[j], received(D_L1IN, j), 1, 1))

    def grad_l1(c):
        gradient(G_L1, c, lambda j: dot(received(R1_OUT, j), hid[j], 1, 1))

    def grad_l2(c):
        gradient(G_L2, c, lambda j: dot(received(R2_OUT, j), cot[j], 1, 1))

    def out_inputs(c):
        return pltpu.make_async_copy(act.at[pl.ds(c * 4, 4)], ginp_h.at[pl.ds(c * 4, 4)], load_sem.at[9 + c])

    def grad_inputs(c):
        def block(i):
            act[c * 4 + i] = dot(r1w[c * 4 + i], received(D_L1IN, c * 4 + i), 1, 0).astype(BF)

        loop(4, block, 4)
        out_inputs(c).start()

    for tc in range(3):
        if tc == 0:
            first[0].wait()
        first[1 + tc].wait()
        if tc == 1:
            for copy in later:
                copy.start()
        produce(D_L2IN, tc, l_w, 1, cot)
        if tc == 0:
            pl.semaphore_wait(barrier, len(mates))
        dispatch(D_L2IN, tc)
    last.start()
    later[0].wait()
    later[1].wait()
    loop(3, lambda tc: produce(R1_OUT, tc, r1w, 0, inp))
    later[2].wait()
    loop(NB, gelu_block)
    later[3].wait()
    last.wait()

    forward(D_L2IN, 0)
    y_own(R1_OUT, 0)

    def step(c):
        arrived(D_L2IN, c)
        d_hidden(c)
        produce(D_L1IN, c, l_w, 1, hid)
        dispatch(D_L1IN, c)

    def follow(c):
        step(c)
        forward(D_L2IN, c + 1)
        y_own(R1_OUT, c + 1)

    loop(2, follow)
    step(2)
    forward(D_L1IN, 0)
    loop(4, grad_r2)
    sends_done(D_L2IN)
    loop(3, lambda tc: produce(R2_OUT, tc, r2w, 0, act))
    forward(D_L1IN, 1)
    z_send(R1_OUT, 0)
    z_send(R1_OUT, 1)
    x_sum(G_R2, 0)
    x_sum(G_R2, 1)
    forward(D_L1IN, 2)
    z_send(R1_OUT, 2)
    dispatch(R1_OUT, 3)
    x_sum(G_R2, 2)
    x_sum(G_R2, 3)
    loop(8, lambda c: z_send(R2_OUT, c))
    loop(3, lambda c: arrived(D_L1IN, c))
    x_done(G_R2)
    loop(4, grad_r1)
    forward(R1_OUT, 0)
    loop(4, grad_inputs)
    forward(R1_OUT, 1)
    y_own(R2_OUT, 0)
    y_own(R2_OUT, 1)
    x_sum(G_R1, 0)
    x_sum(G_R1, 1)
    arrived(R1_OUT, 0)
    grad_l1(0)
    forward(R1_OUT, 2)
    y_own(R2_OUT, 2)
    y_own(R2_OUT, 3)
    x_sum(G_R1, 2)
    x_sum(G_R1, 3)
    arrived(R1_OUT, 1)
    grad_l1(1)
    forward(R1_OUT, 3)
    y_own(R2_OUT, 4)
    x_done(G_R1)
    arrived(R1_OUT, 2)
    grad_l1(2)
    x_sum(G_L1, 0)
    forward(R2_OUT, 0)
    y_own(R2_OUT, 5)
    arrived(R1_OUT, 3)
    grad_l1(3)
    x_sum(G_L1, 1)

    forward(R2_OUT, 1)
    y_own(R2_OUT, 6)
    arrived(R2_OUT, 0)
    grad_l2(0)
    x_sum(G_L1, 2)
    forward(R2_OUT, 2)
    y_own(R2_OUT, 7)
    arrived(R2_OUT, 1)
    grad_l2(1)
    x_sum(G_L1, 3)

    def step(c):
        forward(R2_OUT, c)
        arrived(R2_OUT, c - 1)
        grad_l2(c - 1)
        x_sum(G_L2, c - 3)

    lax.fori_loop(3, 8, lambda c, carry: (step(c), carry)[1], 0)
    x_sum(G_L2, 5)
    arrived(R2_OUT, 7)
    grad_l2(7)
    loop(4, lambda c: finish(G_R2, c))
    x_sum(G_L2, 6)
    x_sum(G_L2, 7)
    for g in (G_R1, G_L1, G_L2):
        loop(SUMS[g], lambda c, g=g: finish(g, c))

    for k in (D_L1IN, R1_OUT, R2_OUT):
        sends_done(k)
    x_done(G_L1)
    x_done(G_L2)
    loop(4, lambda c: out_inputs(c).wait())
    for g in range(4):

        def step(c, g=g):
            await_bytes(zout.at[g, piece(g, c)], ls.at[g, c])
            out_copy(g, c).wait()

        loop(SUMS[g], step)


def deliver(*refs):
    srcs, outs, bufs, (s_in, s_out) = refs[:5], refs[5:10], refs[10:15], refs[15:]
    parts = [(0, pl.ds(c * 4, 4)) for c in range(4)] + [(i, pl.ds(0, NB)) for i in range(1, 5)]
    reads = [
        pltpu.make_async_copy(srcs[i].at[p], bufs[i].at[p], s_in.at[n]) for n, (i, p) in enumerate(parts)
    ]
    writes = [
        pltpu.make_async_copy(bufs[i].at[p], outs[i].at[p], s_out.at[n]) for n, (i, p) in enumerate(parts)
    ]
    for read in reads:
        read.start()
    for read, write in zip(reads, writes):
        read.wait()
        write.start()
    for write in writes:
        write.wait()


def body(inputs, hidden_pre, cotangent, r1_weight, l1_weight, r2_weight, l2_weight):
    anywhere = pl.BlockSpec(memory_space=pl.ANY)
    vmem, dma = pltpu.VMEM, pltpu.SemaphoreType.DMA
    grad = jax.ShapeDtypeStruct((NB, 32, B), F32)
    wide, square = (NB, B, T), (NB, B, B)
    results = pl.pallas_call(
        kernel,
        name="monarch_backward",
        out_shape=(jax.ShapeDtypeStruct(wide, BF), grad, grad, grad, grad),
        in_specs=[anywhere] * 7,
        out_specs=(anywhere,) * 5,
        scratch_shapes=[
            vmem(wide, BF), vmem(wide, BF), vmem(wide, BF),
            vmem(square, BF), vmem(square, BF), vmem(square, BF),
            vmem(wide, BF),
            vmem((3, 16, NB, NB, T), BF),
            vmem((4, 8, NB, NB, T), BF),
            vmem((4, NB, 16, NB, T), BF),
            vmem((2, NB, 2, 4, 32, B), BF),
            vmem((4, 3, NB, 2, 32, B), BF),
            vmem((4, NB, 32, B), BF),
            vmem((4, NB, 32, B), BF),
            vmem((4, NB, 32, B), F32),
            vmem((NB * B, LANES), F32),
            dma((13,)),
        ]
        + [dma((4, 8))] * 10,
        compiler_params=pltpu.CompilerParams(
            collective_id=0, has_side_effects=True, vmem_limit_bytes=67_000_000
        ),
    )(inputs, hidden_pre, cotangent, r1_weight, l1_weight, r2_weight, l2_weight)
    shapes = tuple(jax.ShapeDtypeStruct(r.shape, r.dtype) for r in results)
    return pl.pallas_call(
        deliver,
        name="deliver",
        out_shape=shapes,
        in_specs=[anywhere] * 5,
        out_specs=(anywhere,) * 5,
        scratch_shapes=[vmem(r.shape, r.dtype) for r in results] + [dma((8,)), dma((8,))],
        compiler_params=pltpu.CompilerParams(vmem_limit_bytes=67_000_000),
    )(*results)


def solution(mesh):
    act_spec, weight = P("mp", None, "dp"), P("mp", None, None)
    return jax.shard_map(
        body,
        mesh=mesh,
        in_specs=(act_spec,) * 3 + (weight,) * 4,
        out_specs=(act_spec,) + (P("mp", "dp", None),) * 4,
        check_vma=False,
    )
```
